256 devices in a mesh: ctx: 32 (over z_lo, x, core), wt: 8 (over y, z_hi).
Axes of the slice: x: 4, y: 4, z: 8 (z_hi: 2, z_lo: 4; z = z_hi * 4 + z_lo), core: 2. Of those that a mesh axis runs over, the one named last changes fastest.
Arguments:
- patches: bfloat16 [16384, 1280], P('ctx'), may hold values from -6 to 6
- vit_gain: float32 [1280], replicated, may hold values from 0.5 to 1.5
- vit_codes: bfloat16 [1280, 3, 1280], P(None, None, 'wt'), may hold values from -1 to 1
- vit_scales: bfloat16 [8], P('wt'), may hold values from 0.5 to 2
- vit_bias: float32 [3, 1280], P(None, 'wt'), may hold values from -3 to 3
- window_ids: int32 [16384], P('ctx'), may hold values from 63 to 16383, as said below
- merger_codes: bfloat16 [4, 1280, 8192], P(None, 'wt', 'ctx'), may hold values from -0.078125 to 0.078125
- merger_scales: bfloat16 [1, 8, 8192], P(None, 'wt', 'ctx'), may hold values from 0.5 to 2
- merger_bias: float32 [8192], P('wt'), may hold values from -3 to 3
- positions: int32 [4096], P('ctx'), may hold values from 0 to 16383, as said below
- text_embed: bfloat16 [16384, 8192], P('ctx', 'wt'), may hold values from -6 to 6
- norm_gain: float32 [8192], P('wt'), may hold values from 0.5 to 1.5
- llm_codes: bfloat16 [8192, 8, 768], P('wt', None, 'ctx'), may hold values from -1 to 1
- llm_scales: bfloat16 [8, 8, 768], P('wt', None, 'ctx'), may hold values from 0.5 to 2
- llm_bias: float32 [8, 768], P('wt'), may hold values from -3 to 3
- segments: int32 [16384], P('ctx'), may hold values from 0 to 15, never falling along the last dimension, each value on 1 to 2048 neighbouring positions
Outputs:
- attention_out: bfloat16 [16384, 4096], P('ctx', 'wt')
The draws below stay inside these ranges and needn't reach their ends.
Inputs may be any that keep to these rules, and one draw needn't show every extreme that they name: `window_ids`: windows are runs of consecutive patches of at most 64, never crossing a block of 512 patches; patches of one window share the id, different windows have different ids. `positions`: distinct. The 128 entries of one aligned block (one device's merged tokens) put at most 8 into any one block of 512 positions, and exactly 8 into some block. `segments`: never falling; each run of equal ids is at most 2048 positions long.
All inputs are finite; a program needn't handle non-finite values.
Results may differ from the reference program's by a relative error of at most 0.025.
Values may be sent and summed in bfloat16 or wider, within the bound.
A program may use at most 128 MiB of HBM per device.

```python
import math
import jax
import jax.numpy as jnp
import numpy as np
from jax import lax

VD = 1280
VHD = 80
D = 8192
KVH = 8
HD = 128
GROUP = 4
MERGE = 4
WIN = 64
REACH = 4
P_DEV = 512
C_DEV = 512
IMG_DEV = 128
CAP = 8
PATCHES = 16384
IMG_TOKENS = 4096
TOKENS = 16384
GW = 768
N_CTX = 32
N_WT = 8


def draw_window_ids(key, part):
    shards = PATCHES // P_DEV
    pieces = P_DEV // 4 + 1
    lengths = 4 * jax.random.randint(key, (shards, pieces), 1, WIN // 4 + 1)
    lengths = lengths.at[:, 0].set(WIN)
    end_index = jnp.cumsum(lengths, axis=1)
    patch_index = jnp.arange(P_DEV)
    local = jnp.sum((end_index[:, None, :] <= patch_index[None, :, None]).astype(jnp.int32), axis=2)
    window_end = jnp.take_along_axis(end_index, local, axis=1)
    window_end = jnp.minimum(window_end, P_DEV)
    labels = window_end - 1 + jnp.arange(shards)[:, None] * P_DEV
    return labels.reshape(-1).astype(jnp.int32)


def draw_positions(key, part):
    owners = TOKENS // C_DEV
    group_size = C_DEV // owners
    source_keys = jax.random.split(key, owners)

    def one_source(source_key, source):
        perm_key, lift_key, start_key = jax.random.split(source_key, 3)
        owner_order = jax.random.permutation(perm_key, owners)
        lift_sizes = jax.random.randint(lift_key, (owners // 2,), 0, CAP // 2 + 1)
        lift_sizes = lift_sizes.at[0].set(CAP // 2)
        paired = jnp.stack([CAP // 2 + lift_sizes, CAP // 2 - lift_sizes], axis=1).reshape(-1)
        counts = jnp.zeros((owners,), jnp.int32).at[owner_order].set(paired.astype(jnp.int32))
        starts = jax.random.randint(start_key, (owners,), 0, group_size - counts + 1)
        end_index = jnp.cumsum(counts)
        token_index = jnp.arange(IMG_DEV)
        target = jnp.sum((end_index[None, :] <= token_index[:, None]).astype(jnp.int32), axis=1)
        begin_index = end_index[target] - counts[target]
        return target * C_DEV + source * group_size + starts[target] + token_index - begin_index
    placed = jax.vmap(one_source)(source_keys, jnp.arange(owners))
    return placed.reshape(-1).astype(jnp.int32)


def loguniform_draw(base_key, shape):
    drawn = jax.random.uniform(base_key, shape, jnp.float32, math.log(0.5), math.log(2.0))
    return jnp.exp(drawn)


def draw_patches(key, part):
    noise = jnp.clip(jax.random.normal(jax.random.fold_in(key, 11), (PATCHES, VD), jnp.float32), -6.0, 6.0)
    return jnp.clip(noise, -6.0, 6.0).astype(jnp.bfloat16)


def draw_vit_codes(key, part):
    codes = jnp.clip(jax.random.normal(jax.random.fold_in(key, 21), (VD, 3, VD), jnp.float32), -6.0, 6.0) * VD ** (-0.5)
    return jnp.clip(codes, -1.0, 1.0).astype(jnp.bfloat16)


def draw_vit_scales(key, part):
    scales = loguniform_draw(jax.random.fold_in(key, 31), (N_WT,))
    return scales.astype(jnp.bfloat16)


def draw_text_embed(key, part):
    noise = jnp.clip(jax.random.normal(jax.random.fold_in(key, 41), (TOKENS, D), jnp.float32), -6.0, 6.0)
    return jnp.clip(noise, -6.0, 6.0).astype(jnp.bfloat16)


def draw_llm_codes(key, part):
    codes = jnp.clip(jax.random.normal(jax.random.fold_in(key, 51), (D, KVH, GW), jnp.float32), -6.0, 6.0) * D ** (-0.5)
    return jnp.clip(codes, -1.0, 1.0).astype(jnp.bfloat16)


def draw_llm_scales(key, part):
    scales = loguniform_draw(jax.random.fold_in(key, 61), (N_WT, KVH, GW))
    return scales.astype(jnp.bfloat16)


def steps_of(key, extent, cuts, low, high):
    loudness = 1.0
    for axis_at, parts in cuts:
        heights = jax.random.uniform(jax.random.fold_in(jax.random.fold_in(key, 6), axis_at), (parts,), jnp.float32, low / len(cuts), high / len(cuts))
        loudness = loudness * jnp.repeat(jnp.exp(heights), extent[axis_at] // parts).reshape((-1,) + (1,) * (len(extent) - 1 - axis_at))
    return loudness


def split_up(count, total, reach, slope):
    portions = [(1 << 20) // math.isqrt(standing ** slope) + 1 for standing in range(2, count + 1)]
    spare, holding = total - reach - (count - 1), [1] * (count - 1)
    while spare > 0:
        candidates = [i for i in range(count - 1) if holding[i] < reach]
        whole, left = sum([portions[i] for i in candidates]), spare
        for i in candidates:
            extra = min(reach - holding[i], max(1, left * portions[i] // whole), spare)
            holding[i] = holding[i] + extra
            spare = spare - extra
    return np.array([reach] + holding)


def ragged(key, number_of, total, limit, lean):
    if number_of == 2:
        one = jax.random.randint(key, (), max(1, total - limit), min(limit, total - 1) + 1)
        return jnp.stack([one, total - one])
    sizes = jnp.asarray(split_up(number_of, total, limit, lean), jnp.int32)
    couples = (number_of - 1) // 2
    source_of, sink = sizes[1:1 + 2 * couples:2], sizes[2:2 + 2 * couples:2]
    slack = jnp.minimum(source_of - 1, limit - sink)
    moved = jax.random.randint(jax.random.fold_in(key, 1), (couples,), 0, 1 << 20) % (slack + 1)
    sizes = sizes.at[1:1 + 2 * couples:2].set(source_of - moved).at[2:2 + 2 * couples:2].set(sink + moved)
    return sizes[jax.random.permutation(jax.random.fold_in(key, 2), number_of)]


def bell_draw(own_key, dims, spread, most, cuts=(), kind=jnp.bfloat16):
    values = jax.random.normal(own_key, dims, jnp.float32) * spread
    if len(cuts) > 0:
        values = steps_of(own_key, dims, cuts, -0.22, 0.18) * values
    return jnp.clip(values, min=-most, max=most).astype(kind)


def setup_inputs(seed: int = 0) -> dict:
    key_list = jax.random.split(jax.random.key(seed), 17)
    return {
        "patches": draw_patches(jax.random.fold_in(key_list[16], 71), 0),
        "vit_gain": jnp.clip(1.0 + 0.1 * jax.random.normal(key_list[1], (VD,), jnp.float32), 0.5, 1.5),
        "vit_codes": draw_vit_codes(jax.random.fold_in(key_list[16], 71), 0),
        "vit_scales": draw_vit_scales(jax.random.fold_in(key_list[16], 71), 0),
        "vit_bias": bell_draw(key_list[4], (3, VD), 0.5, 3.0, ((1, 8),), jnp.float32),
        "window_ids": draw_window_ids(jax.random.fold_in(key_list[16], 71), 0),
        "merger_codes": bell_draw(key_list[6], (MERGE, VD, D), (MERGE * VD) ** -0.5, 0.078125, ((1, 8), (2, 32))),
        "merger_scales": jnp.clip(jnp.exp(math.log(2.0) - 1.3862944 * jax.random.uniform(key_list[7], (1, N_WT, D), jnp.float32) ** steps_of(key_list[7], (1, N_WT, D), ((1, 8), (2, 32)), -0.2, 0.2)), 0.5, 2.0).astype(jnp.bfloat16),
        "merger_bias": bell_draw(key_list[8], (D,), 0.5, 3.0, ((0, 8),), jnp.float32),
        "positions": draw_positions(jax.random.fold_in(key_list[16], 71), 0),
        "text_embed": draw_text_embed(jax.random.fold_in(key_list[16], 71), 0),
        "norm_gain": jnp.clip(1.0 + 0.1 * jax.random.normal(key_list[11], (D,), jnp.float32), 0.5, 1.5),
        "llm_codes": draw_llm_codes(jax.random.fold_in(key_list[16], 71), 0),
        "llm_scales": draw_llm_scales(jax.random.fold_in(key_list[16], 71), 0),
        "llm_bias": bell_draw(key_list[14], (KVH, GW), 0.5, 3.0, ((0, 8),), jnp.float32),
        "segments": jnp.searchsorted(jnp.cumsum(ragged(key_list[15], TOKENS // (2 * C_DEV), TOKENS, REACH * C_DEV, 1)), jnp.arange(TOKENS), side="right").astype(jnp.int32),
    }


VIT_EPS = 1e-06
RMS_EPS = 1e-06
ROPE_BASE = 1000000.0
FILL_LOW = -1e+30

def softmax_rows(scores, allowed):
    masked = jnp.where(allowed, scores, FILL_LOW)
    highest = lax.optimization_barrier(jnp.max(masked, axis=-1, keepdims=True))
    raised = jnp.exp(masked - highest)
    return raised / lax.optimization_barrier(jnp.sum(raised, axis=-1, keepdims=True))

def vision_norm_rows(patches, vit_gain):
    values = patches.astype(jnp.float32)
    mean_square = lax.optimization_barrier(jnp.mean(values * values, axis=1, keepdims=True))
    return (values * lax.rsqrt(mean_square + VIT_EPS) * vit_gain).astype(jnp.bfloat16)

def window_attention(normed, weight_block, bias_block, window_ids):
    row_count = normed.shape[0]
    packed = jnp.dot(normed, weight_block.reshape(normed.shape[1], -1), preferred_element_type=jnp.float32)
    triple = (packed.reshape(row_count, 3, -1) + bias_block).astype(jnp.bfloat16)
    heads_here = triple.shape[2] // VHD
    queries = triple[:, 0].reshape(row_count, heads_here, VHD).astype(jnp.float32)
    keys_here = triple[:, 1].reshape(row_count, heads_here, VHD).astype(jnp.float32)
    values_here = triple[:, 2].reshape(row_count, heads_here, VHD).astype(jnp.float32)
    scores = jnp.einsum('qhd,khd->hqk', queries, keys_here) * VHD ** (-0.5)
    allowed = window_ids[:, None] == window_ids[None, :]
    softmaxed = softmax_rows(scores, allowed[None]).astype(jnp.bfloat16)
    blended = jnp.einsum('hqk,khd->qhd', softmaxed.astype(jnp.float32), values_here)
    return blended.astype(jnp.bfloat16).reshape(row_count, -1)

def rope_tables(first, length):
    places = (first + jnp.arange(length, dtype=jnp.int32)).astype(jnp.float32)
    frequency = ROPE_BASE ** (-jnp.arange(0, HD, 2).astype(jnp.float32) / HD)
    angles = places[:, None] * frequency[None, :]
    angles = jnp.concatenate([angles, angles], axis=1)
    return (jnp.cos(angles), jnp.sin(angles))

def rotary(inputs, cosine, sine):
    halfway = inputs.shape[-1] // 2
    turned = jnp.concatenate([-inputs[..., halfway:], inputs[..., :halfway]], axis=-1)
    return inputs * cosine + turned * sine

def split_heads(triple, cosine, sine):
    row_count, group_count = (triple.shape[0], triple.shape[1])
    queries = triple[:, :, :GROUP * HD].reshape(row_count, group_count, GROUP, HD)
    queries = rotary(queries, cosine[:, None, None, :], sine[:, None, None, :]).astype(jnp.bfloat16)
    keys_rot = rotary(triple[:, :, GROUP * HD:(GROUP + 1) * HD], cosine[:, None, :], sine[:, None, :]).astype(jnp.bfloat16)
    values_cut = triple[:, :, (GROUP + 1) * HD:].astype(jnp.bfloat16)
    return (queries, keys_rot, values_cut)

def reference(patches, vit_gain, vit_codes, vit_scales, vit_bias, window_ids, merger_codes, merger_scales, merger_bias, positions, text_embed, norm_gain, llm_codes, llm_scales, llm_bias, segments):
    vit_cols = vit_codes.shape[2] // N_WT
    vit_weight = (vit_codes.astype(jnp.float32) * jnp.repeat(vit_scales.astype(jnp.float32), vit_cols)).astype(jnp.bfloat16)
    normed_patches = vision_norm_rows(patches, vit_gain)
    patch_blocks = normed_patches.reshape(N_CTX, P_DEV, VD)
    window_blocks = window_ids.reshape(N_CTX, P_DEV)
    attended = lax.map(lambda pair: window_attention(pair[0], vit_weight, vit_bias, pair[1]), (patch_blocks, window_blocks))
    attended = attended.reshape(IMG_TOKENS, MERGE, N_WT, VD // N_WT)
    merger_weight = (merger_codes.astype(jnp.float32) * jnp.repeat(merger_scales.astype(jnp.float32), VD // N_WT, axis=1)).astype(jnp.bfloat16)
    merger_weight = merger_weight.reshape(MERGE, N_WT, VD // N_WT, D)
    merger_total = jnp.zeros((IMG_TOKENS, D), jnp.float32)
    for shard_index in range(N_WT):
        partial_value = jnp.dot(attended[:, :, shard_index].reshape(IMG_TOKENS, -1), merger_weight[:, shard_index].reshape(-1, D), preferred_element_type=jnp.float32)
        merger_total = merger_total + lax.optimization_barrier(partial_value.astype(jnp.bfloat16)).astype(jnp.float32)
    merged_embed = (merger_total + merger_bias).astype(jnp.bfloat16)
    hidden = text_embed.at[positions].set(merged_embed)
    values = hidden.astype(jnp.float32)
    mean_square = lax.optimization_barrier(jnp.mean(values * values, axis=1, keepdims=True))
    normed = (values * lax.rsqrt(mean_square + RMS_EPS) * norm_gain).astype(jnp.bfloat16)
    rows_wt = D // N_WT
    llm_weight = (llm_codes.astype(jnp.float32) * jnp.repeat(llm_scales.astype(jnp.float32), rows_wt, axis=0)).astype(jnp.bfloat16)
    projected = jnp.zeros((TOKENS, KVH * GW), jnp.float32)
    for shard_index in range(N_WT):
        partial_value = jnp.dot(normed[:, shard_index * rows_wt:(shard_index + 1) * rows_wt], llm_weight[shard_index * rows_wt:(shard_index + 1) * rows_wt].reshape(rows_wt, -1), preferred_element_type=jnp.float32)
        projected = projected + lax.optimization_barrier(partial_value.astype(jnp.bfloat16)).astype(jnp.float32)
    triple = projected.reshape(TOKENS, KVH, GW) + llm_bias
    cosine, sine = rope_tables(0, TOKENS)
    queries, keys_rot, values_cut = split_heads(triple, cosine, sine)
    padding = REACH * C_DEV
    window_len = (REACH + 1) * C_DEV
    keys_pad = jnp.concatenate([jnp.zeros((padding, KVH, HD), jnp.bfloat16), keys_rot], axis=0)
    values_pad = jnp.concatenate([jnp.zeros((padding, KVH, HD), jnp.bfloat16), values_cut], axis=0)
    segments_pad = jnp.concatenate([jnp.zeros((padding,), jnp.int32), segments], axis=0)
    places_pad = jnp.arange(TOKENS + padding, dtype=jnp.int32) - padding

    def attend_block(block_index):
        first_row = (block_index * C_DEV).astype(jnp.int32)
        query_rows = lax.dynamic_slice_in_dim(queries, first_row, C_DEV, 0)
        query_segments = lax.dynamic_slice_in_dim(segments, first_row, C_DEV, 0)
        key_rows = lax.dynamic_slice_in_dim(keys_pad, first_row, window_len, 0)
        value_rows = lax.dynamic_slice_in_dim(values_pad, first_row, window_len, 0)
        key_segments = lax.dynamic_slice_in_dim(segments_pad, first_row, window_len, 0)
        key_places = lax.dynamic_slice_in_dim(places_pad, first_row, window_len, 0)
        query_places = first_row + jnp.arange(C_DEV, dtype=jnp.int32)
        allowed = (query_segments[:, None] == key_segments[None, :]) & (key_places[None, :] <= query_places[:, None]) & (key_places[None, :] >= 0)
        scores = jnp.einsum('qgjd,kgd->gjqk', query_rows.astype(jnp.float32), key_rows.astype(jnp.float32)) * HD ** (-0.5)
        softmaxed = softmax_rows(scores, allowed[None, None]).astype(jnp.bfloat16)
        blended = jnp.einsum('gjqk,kgd->qgjd', softmaxed.astype(jnp.float32), value_rows.astype(jnp.float32))
        return blended.astype(jnp.bfloat16).reshape(C_DEV, -1)
    result = lax.map(attend_block, jnp.arange(N_CTX, dtype=jnp.int32))
    return result.reshape(TOKENS, -1)
```

```python
import functools

import jax
import jax.numpy as jnp
from jax import lax
from jax.experimental import pallas as pl
from jax.experimental.pallas import tpu as pltpu
from jax.sharding import PartitionSpec as P

VHD = 80
D = 8192
KVH = 8
HD = 128
GROUP = 4
MERGE = 4
REACH = 4
CAP = 8

VIT_EPS = 1e-06
RMS_EPS = 1e-06
ROPE_BASE = 1000000.0
FILL_LOW = -1e30

NX = 4
NZ = 4
NY = 4
BF = jnp.bfloat16
F32 = jnp.float32


def here():
    c = lax.axis_index("ctx")
    w = lax.axis_index("wt")
    return {"z": c // 8, "x": (c // 2) % 4, "k": c % 2, "y": w // 2, "h": w % 2}


def device_of(at):
    return {"ctx": at["z"] * 8 + at["x"] * 2 + at["k"], "wt": at["y"] * 2 + at["h"]}


SIZES = {"z": 4, "x": 4, "k": 2, "y": 4, "h": 2}


def moved(at, **offsets):
    new = dict(at)
    for name, offset in offsets.items():
        new[name] = (at[name] + offset) % SIZES[name]
    return new


class Net:
    def __init__(self, send_sems, recv_sems, local_sems):
        self.send_sems, self.recv_sems, self.local_sems = send_sems, recv_sems, local_sems
        self.sent, self.kept = [], []

    def send(self, src, dst, to):
        i = len(self.sent)
        copy = pltpu.make_async_remote_copy(
            src_ref=src,
            dst_ref=dst,
            send_sem=self.send_sems.at[i],
            recv_sem=self.recv_sems.at[i],
            device_id=device_of(to),
            device_id_type=pl.DeviceIdType.MESH,
        )
        copy.start()
        self.sent.append([copy, False])
        return i

    def local(self, src, dst):
        copy = pltpu.make_async_copy(src, dst, self.local_sems.at[len(self.kept)])
        copy.start()
        self.kept.append(copy)

    def arrived(self, i):
        if not self.sent[i][1]:
            self.sent[i][0].wait_recv()
            self.sent[i][1] = True

    def finish(self):
        for copy in self.kept:
            copy.wait()
        for i in range(len(self.sent)):
            self.arrived(i)
        for copy, _ in self.sent:
            copy.wait_send()


def greet(peers):
    barrier = pltpu.get_barrier_semaphore()
    for peer in peers:
        pl.semaphore_signal(
            barrier, inc=1, device_id=device_of(peer), device_id_type=pl.DeviceIdType.MESH
        )
    pl.semaphore_wait(barrier, len(peers))


def exchange(name, cid, body, peers, in_spaces, ins, outs, aliases, sends, locals_=1):
    def kernel(*refs):
        in_refs = refs[: len(ins)]
        out_refs = refs[len(ins) : len(ins) + len(outs)]
        send_sems, recv_sems, local_sems = refs[len(ins) + len(outs) :]
        at = here()
        greet(peers(at))
        net = Net(send_sems, recv_sems, local_sems)
        body(at, net, in_refs, out_refs)
        net.finish()

    return pl.pallas_call(
        kernel,
        out_shape=outs,
        in_specs=[pl.BlockSpec(memory_space=s) for s in in_spaces],
        out_specs=[pl.BlockSpec(memory_space=pltpu.HBM) for _ in outs],
        scratch_shapes=[
            pltpu.SemaphoreType.DMA((sends,)),
            pltpu.SemaphoreType.DMA((sends,)),
            pltpu.SemaphoreType.DMA((max(1, locals_),)),
        ],
        input_output_aliases=aliases,
        compiler_params=pltpu.CompilerParams(collective_id=cid, has_side_effects=True),
        name=name,
    )(*ins)


V = pltpu.VMEM
H = pltpu.HBM
LEFT = (1, 2, 3)
T1, T2 = 256, 384


def spread(features, places, merger_piece, llm_piece, bias_rows, text):
    tokens, depth = features.shape
    cols = merger_piece.shape[0]
    heads2, wide, rows = llm_piece.shape[1:]

    def peers(at):
        return (
            [moved(at, z=d) for d in LEFT]
            + [moved(at, x=d) for d in LEFT]
            + [moved(at, y=d) for d in LEFT]
            + [moved(at, k=1)]
        )

    def body(at, net, i, o):
        feat, place, merger, llm, bias, txt = i
        feat_all, place_all, merger_all, bias_all, llm_all, txt_all = o
        z, x, k, y = at["z"], at["x"], at["k"], at["y"]
        mine = x * 2 + k
        passing = []
        for d in LEFT:
            net.send(feat, feat_all.at[z], moved(at, z=d))
            net.send(place, place_all.at[z], moved(at, z=d))
            passing.append(net.send(merger, merger_all.at[mine], moved(at, x=d)))
            to = moved(at, y=d)
            net.send(llm.at[to["y"]], llm_all.at[y, :, z, x, k], to)
            net.send(bias, bias_all.at[y], to)
        net.send(merger, merger_all.at[mine], moved(at, k=1))
        for d in LEFT:
            net.send(txt.at[:T1], txt_all.at[y, :T1], moved(at, y=d))
        net.local(feat, feat_all.at[z])
        net.local(place, place_all.at[z])
        net.local(merger, merger_all.at[mine])
        net.local(llm.at[y], llm_all.at[y, :, z, x, k])
        net.local(bias, bias_all.at[y])
        net.local(txt, txt_all.at[y])
        for d, n in zip(LEFT, passing):
            net.arrived(n)
            source = ((x + 4 - d) % 4) * 2 + k
            net.send(merger_all.at[source], merger_all.at[source], moved(at, k=1))

    sds = jax.ShapeDtypeStruct
    return exchange(
        "spread",
        1,
        body,
        peers,
        [V] * 6,
        (features, places, merger_piece, llm_piece, bias_rows, text),
        (
            sds((NZ, tokens, depth), BF),
            sds((NZ,) + places.shape, jnp.int32),
            sds((NX * 2, cols, depth), BF),
            sds((NY,) + bias_rows.shape, F32),
            sds((NY, heads2, NZ, NX, 2, wide, rows), BF),
            sds((NY,) + text.shape, BF),
        ),
        {},
        15 + 1 + 3 + 3,
        6,
    )


def reduce_y(partial, llm_all):
    def peers(at):
        return [moved(at, y=d) for d in LEFT] + [moved(at, z=d) for d in LEFT]

    def body(at, net, i, o):
        part, _ = i
        got, llm = o
        z, x, k = at["z"], at["x"], at["k"]
        for d in LEFT:
            to = moved(at, y=d)
            net.send(part.at[to["y"]], got.at[d - 1], to)
        for d in LEFT:
            net.send(llm.at[:, :, z, x, k], llm.at[:, :, z, x, k], moved(at, z=d))

    sds = jax.ShapeDtypeStruct
    return exchange(
        "reduce_y",
        2,
        body,
        peers,
        [V, H],
        (partial, llm_all),
        (sds((3,) + partial.shape[1:], BF), sds(llm_all.shape, BF)),
        {1: 1},
        6,
    )


def reduce_h(half, llm_all, text, txt_all):
    def peers(at):
        return (
            [moved(at, h=1)]
            + [moved(at, x=d) for d in (1, 3)]
            + [moved(at, y=d) for d in LEFT]
        )

    def body(at, net, i, o):
        part, _, txt, _ = i
        got, llm, txt_all_ = o
        x, k, y = at["x"], at["k"], at["y"]
        net.send(part, got, moved(at, h=1))
        for d in (1, 3):
            piece = llm.at[:, :, pl.ds(0, 2), x, k]
            net.send(piece, piece, moved(at, x=d))
        for d in LEFT:
            net.send(txt.at[T1:T2], txt_all_.at[y, T1:T2], moved(at, y=d))

    sds = jax.ShapeDtypeStruct
    return exchange(
        "reduce_h",
        3,
        body,
        peers,
        [V, H, V, H],
        (half, llm_all, text, txt_all),
        (sds(half.shape, BF), sds(llm_all.shape, BF), sds(txt_all.shape, BF)),
        {1: 1, 3: 2},
        6,
    )


OTHERS = [(a, b, e) for a in range(4) for b in range(4) for e in range(2) if (a, b, e) != (0, 0, 0)]


def route(packed, llm_all, text, txt_all):
    def peers(at):
        return [moved(at, z=a, x=b, k=e) for a, b, e in OTHERS] + [moved(at, y=d) for d in LEFT]

    def body(at, net, i, o):
        pack, _, txt, _ = i
        got, llm, txt_all_ = o
        z, x, k, y = at["z"], at["x"], at["k"], at["y"]
        mine = got.at[z, x * 2 + k]
        for a, b, e in OTHERS:
            to = moved(at, z=a, x=b, k=e)
            net.send(pack.at[to["z"] * 8 + to["x"] * 2 + to["k"]], mine, to)
        for d in (1, 3):
            piece = llm.at[:, :, pl.ds(2, 2), x, k]
            net.send(piece, piece, moved(at, x=d))
        for d in LEFT:
            net.send(txt.at[T2:], txt_all_.at[y, T2:], moved(at, y=d))
        net.local(pack.at[z * 8 + x * 2 + k], mine)

    sds = jax.ShapeDtypeStruct
    return exchange(
        "route",
        4,
        body,
        peers,
        [V, H, V, H],
        (packed, llm_all, text, txt_all),
        (
            sds((NZ, NX * 2) + packed.shape[1:], BF),
            sds(llm_all.shape, BF),
            sds(txt_all.shape, BF),
        ),
        {1: 1, 3: 2},
        len(OTHERS) + 5,
    )


def collect(image, llm_all):
    def peers(at):
        return (
            [moved(at, y=d) for d in LEFT] + [moved(at, x=d) for d in (1, 3)] + [moved(at, k=1)]
        )

    def body(at, net, i, o):
        img, _ = i
        got, llm = o
        x, k, y = at["x"], at["k"], at["y"]
        for d in LEFT:
            net.send(img, got.at[:, y], moved(at, y=d))
        far = []
        for d, first in ((1, 0), (3, 2)):
            piece = llm.at[:, :, pl.ds(first, 2), (x + 4 - d) % 4, k]
            far.append(net.send(piece, piece, moved(at, x=d)))
        for step in (0, 1, 3):
            piece = llm.at[:, :, :, (x + step) % 4, k]
            net.send(piece, piece, moved(at, k=1))
        net.local(img, got.at[:, y])
        for n, first in zip(far, (0, 2)):
            net.arrived(n)
            piece = llm.at[:, :, pl.ds(first, 2), (x + 2) % 4, k]
            net.send(piece, piece, moved(at, k=1))

    sds = jax.ShapeDtypeStruct
    return exchange(
        "collect",
        5,
        body,
        peers,
        [V, H],
        (image, llm_all),
        (sds((image.shape[0], NY) + image.shape[1:], BF), sds(llm_all.shape, BF)),
        {1: 1},
        3 + 2 + 3 + 2,
    )


def reduce_qkv(part, squares):
    def peers(at):
        return [moved(at, h=1)]

    def body(at, net, i, o):
        for src, dst in zip(i, o):
            net.send(src, dst, moved(at, h=1))

    sds = jax.ShapeDtypeStruct
    return exchange(
        "reduce_qkv",
        6,
        body,
        peers,
        [V, V],
        (part, squares),
        (sds(part.shape, BF), sds(squares.shape, F32)),
        {},
        2,
    )


def ahead(at, steps):
    place = (at["z"] * 8 + at["x"] * 2 + at["k"] + 32 + steps) % 32
    return {"z": place // 8, "x": (place // 2) % 4, "k": place % 2, "y": at["y"], "h": at["h"]}


def halo(kv, segs):
    def peers(at):
        return [ahead(at, s) for s in (1, 2, 3, 4, -1, -2, -3, -4)]

    def body(at, net, i, o):
        kv_in, seg_in = i
        kv_out, seg_out = o
        for s in range(1, REACH + 1):
            net.send(kv_in, kv_out.at[s], ahead(at, s))
            net.send(seg_in, seg_out.at[s], ahead(at, s))
        net.local(kv_in, kv_out.at[0])
        net.local(seg_in, seg_out.at[0])

    sds = jax.ShapeDtypeStruct
    return exchange(
        "halo",
        7,
        body,
        peers,
        [V, V],
        (kv, segs),
        (sds((REACH + 1,) + kv.shape, BF), sds((REACH + 1,) + segs.shape, jnp.int32)),
        {},
        2 * REACH,
        2,
    )


def softmax_rows(scores, allowed):
    masked = jnp.where(allowed, scores, FILL_LOW)
    highest = jnp.max(masked, axis=-1, keepdims=True)
    raised = jnp.exp(masked - highest)
    return raised / jnp.sum(raised, axis=-1, keepdims=True)


def vision_norm_rows(patches, vit_gain):
    values = patches.astype(F32)
    mean_square = jnp.mean(values * values, axis=1, keepdims=True)
    return (values * lax.rsqrt(mean_square + VIT_EPS) * vit_gain).astype(BF)


def window_attention(normed, weight_block, bias_block, window_ids):
    row_count = normed.shape[0]
    packed = jnp.dot(
        normed, weight_block.reshape(normed.shape[1], -1), preferred_element_type=F32
    )
    triple = (packed.reshape(row_count, 3, -1) + bias_block).astype(BF)
    heads_here = triple.shape[2] // VHD
    queries = triple[:, 0].reshape(row_count, heads_here, VHD)
    keys_here = triple[:, 1].reshape(row_count, heads_here, VHD)
    values_here = triple[:, 2].reshape(row_count, heads_here, VHD)
    scores = jnp.einsum(
        "qhd,khd->hqk", queries, keys_here, preferred_element_type=F32
    ) * VHD ** (-0.5)
    allowed = window_ids[:, None] == window_ids[None, :]
    softmaxed = softmax_rows(scores, allowed[None]).astype(BF)
    blended = jnp.einsum("hqk,khd->qhd", softmaxed, values_here, preferred_element_type=F32)
    return blended.astype(BF).reshape(row_count, -1)


def rope_tables(first, length):
    places = (first + jnp.arange(length, dtype=jnp.int32)).astype(F32)
    frequency = ROPE_BASE ** (-jnp.arange(0, HD, 2).astype(F32) / HD)
    angles = places[:, None] * frequency[None, :]
    angles = jnp.concatenate([angles, angles], axis=1)
    return (jnp.cos(angles), jnp.sin(angles))


def rotary(inputs, cosine, sine):
    halfway = inputs.shape[-1] // 2
    turned = jnp.concatenate([-inputs[..., halfway:], inputs[..., :halfway]], axis=-1)
    return inputs * cosine + turned * sine


def pack_tokens(values, positions, span, owners):
    items = values.shape[0]
    target = positions // span
    item_order = jnp.arange(items, dtype=jnp.int32)
    before = (target[None, :] == target[:, None]) & (item_order[None, :] < item_order[:, None])
    ranks = jnp.sum(before.astype(jnp.int32), axis=1)
    slots = target * CAP + ranks
    table = slots[None, :] == jnp.arange(owners * CAP, dtype=jnp.int32)[:, None]
    local = positions - target * span
    lanes = jnp.arange(HD)[None, :]
    notes = jnp.where(lanes == 0, (local // 16)[:, None], (local % 16)[:, None])
    notes = jnp.where(lanes == 2, 1, notes)
    rows = jnp.concatenate([values, notes.astype(BF)], axis=1)
    packed = jnp.dot(table.astype(BF), rows, preferred_element_type=F32).astype(BF)
    return packed.reshape(owners, CAP, rows.shape[1])


def project(hidden, weights):
    blocks = [
        lax.dot_general(
            hidden[b],
            weights[b],
            (((1,), (1,)), ((), ())),
            preferred_element_type=F32,
        )
        for b in range(hidden.shape[0])
    ]
    return (blocks[0] + blocks[1]) + (blocks[2] + blocks[3])


def on_device(
    patches,
    vit_gain,
    vit_codes,
    vit_scales,
    vit_bias,
    window_ids,
    merger_codes,
    merger_scales,
    merger_bias,
    positions,
    text_embed,
    norm_gain,
    llm_codes,
    llm_scales,
    llm_bias,
    segments,
):
    at = here()
    owners = lax.axis_size("ctx")
    row_count, width = text_embed.shape
    first = lax.axis_index("ctx") * row_count

    llm_weight = (llm_codes.astype(F32) * llm_scales.astype(F32)).astype(BF)
    llm_weight = (llm_weight.astype(F32) * norm_gain[:, None, None]).astype(BF)
    llm_piece = jnp.transpose(llm_weight, (1, 2, 0)).reshape(NY, 2, -1, width)
    merger_weight = (merger_codes.astype(F32) * merger_scales.astype(F32)).astype(BF)
    merger_piece = merger_weight.reshape(-1, merger_weight.shape[2]).T

    normed_patches = vision_norm_rows(patches, vit_gain)
    vit_weight = (vit_codes.astype(F32) * vit_scales.astype(F32)[0]).astype(BF)
    attended = window_attention(normed_patches, vit_weight, vit_bias, window_ids)
    token_count = positions.shape[0]
    features = attended.reshape(token_count, -1)
    place_rows = jnp.broadcast_to(positions[None, :], (8, token_count))

    feat_all, place_all, merger_all, bias_all, llm_all, txt_all = spread(
        features, place_rows, merger_piece, llm_piece, merger_bias.reshape(8, -1), text_embed
    )
    product = lax.dot_general(
        feat_all.reshape(-1, feat_all.shape[2]),
        merger_all.reshape(-1, merger_all.shape[2]),
        (((1,), (1,)), ((), ())),
        preferred_element_type=F32,
    ).astype(BF)
    product = product.reshape(NZ, token_count, -1)
    got, llm_all = reduce_y(product, llm_all)
    total = lax.dynamic_index_in_dim(product, at["y"], 0, keepdims=False).astype(F32)
    total = total + got.astype(F32).sum(axis=0)
    low, high = (total[:, :width], total[:, width:])
    is_high = at["h"] == 1
    keep = jnp.where(is_high, high, low)
    give = jnp.where(is_high, low, high).astype(BF)
    got, llm_all, txt_all = reduce_h(give, llm_all, text_embed, txt_all)
    bias_here = lax.dynamic_index_in_dim(bias_all, at["z"], 0, keepdims=False).reshape(-1)
    merged = (keep + got.astype(F32) + bias_here).astype(BF)
    places_here = lax.dynamic_index_in_dim(place_all, at["y"], 0, keepdims=False)[0]
    packed = pack_tokens(merged, places_here, row_count, owners)
    image, llm_all, txt_all = route(packed, llm_all, text_embed, txt_all)
    image = image.reshape(NZ, -1, image.shape[3])
    slots, llm_all = collect(image, llm_all)
    slots = slots.reshape(NZ, -1, slots.shape[3])

    notes = slots[0, :, width : width + 3].astype(F32)
    local = jnp.where(notes[:, 2] > 0.5, notes[:, 0] * 16.0 + notes[:, 1], -1.0).astype(jnp.int32)
    table = local[None, :] == jnp.arange(row_count, dtype=jnp.int32)[:, None]
    filled = jnp.stack(
        [
            jnp.dot(table.astype(BF), slots[b, :, :width], preferred_element_type=F32).astype(BF)
            for b in range(NY)
        ]
    )
    covered = jnp.any(table, axis=1)
    hidden = jnp.where(covered[None, :, None], filled, txt_all)
    raised = hidden.astype(F32)
    squares = jnp.sum(raised * raised, axis=(0, 2))
    weights = llm_all.reshape(NY, -1, width)
    partial_sum = project(hidden, weights)
    columns = partial_sum.shape[1] // 2
    low, high = (partial_sum[:, :columns], partial_sum[:, columns:])
    keep = jnp.where(is_high, high, low)
    give = jnp.where(is_high, low, high).astype(BF)
    square_rows = squares.reshape(-1, 128)
    got, got_squares = reduce_qkv(give, square_rows)
    scale = lax.rsqrt((squares + got_squares.reshape(-1)) / D + RMS_EPS)
    triple = (keep + got.astype(F32)) * scale[:, None] + llm_bias

    cosine, sine = rope_tables(first, row_count)
    queries = rotary(
        triple[:, : GROUP * HD].reshape(row_count, GROUP, HD), cosine[:, None], sine[:, None]
    ).astype(BF)
    keys_rot = rotary(triple[:, GROUP * HD : (GROUP + 1) * HD], cosine, sine).astype(BF)
    values_cut = triple[:, (GROUP + 1) * HD :].astype(BF)
    kv_all, seg_all = halo(
        jnp.concatenate([keys_rot, values_cut], axis=1), segments.reshape(-1, 128)
    )
    keys_all = kv_all[:, :, :HD].reshape(-1, HD)
    values_all = kv_all[:, :, HD:].reshape(-1, HD)
    key_segments = seg_all.reshape(-1)
    key_places = jnp.concatenate(
        [
            first - distance * row_count + jnp.arange(row_count, dtype=jnp.int32)
            for distance in range(REACH + 1)
        ],
        axis=0,
    )
    query_places = first + jnp.arange(row_count, dtype=jnp.int32)
    allowed = (
        (segments[:, None] == key_segments[None, :])
        & (key_places[None, :] <= query_places[:, None])
        & (key_places[None, :] >= 0)
    )
    scores = jnp.einsum(
        "qjd,kd->jqk", queries, keys_all, preferred_element_type=F32
    ) * HD ** (-0.5)
    softmaxed = softmax_rows(scores, allowed[None]).astype(BF)
    blended = jnp.einsum("jqk,kd->qjd", softmaxed, values_all, preferred_element_type=F32)
    return blended.astype(BF).reshape(row_count, -1)


def solution(mesh):
    in_specs = (
        P("ctx", None),
        P(),
        P(None, None, "wt"),
        P("wt"),
        P(None, "wt"),
        P("ctx"),
        P(None, "wt", "ctx"),
        P(None, "wt", "ctx"),
        P("wt"),
        P("ctx"),
        P("ctx", "wt"),
        P("wt"),
        P("wt", None, "ctx"),
        P("wt", None, "ctx"),
        P("wt", None),
        P("ctx"),
    )
    out_specs = P("ctx", "wt")
    return jax.shard_map(
        on_device, mesh=mesh, in_specs=in_specs, out_specs=out_specs, check_vma=False
    )
```

```python
import functools

import jax
import jax.numpy as jnp
from jax import lax
from jax.experimental import pallas as pl
from jax.experimental.pallas import tpu as pltpu
from jax.sharding import PartitionSpec as P

VHD = 80
D = 8192
KVH = 8
HD = 128
GROUP = 4
MERGE = 4
REACH = 4
CAP = 8

VIT_EPS = 1e-06
RMS_EPS = 1e-06
ROPE_BASE = 1000000.0
FILL_LOW = -1e30

NX = 4
NZ = 4
NY = 4
BF = jnp.bfloat16
F32 = jnp.float32


def here():
    c = lax.axis_index("ctx")
    w = lax.axis_index("wt")
    return {"z": c // 8, "x": (c // 2) % 4, "k": c % 2, "y": w // 2, "h": w % 2}


def device_of(at):
    return {"ctx": at["z"] * 8 + at["x"] * 2 + at["k"], "wt": at["y"] * 2 + at["h"]}


SIZES = {"z": 4, "x": 4, "k": 2, "y": 4, "h": 2}


def moved(at, **offsets):
    new = dict(at)
    for name, offset in offsets.items():
        new[name] = (at[name] + offset) % SIZES[name]
    return new


class Net:
    def __init__(self, send_sems, recv_sems, local_sems):
        self.send_sems, self.recv_sems, self.local_sems = send_sems, recv_sems, local_sems
        self.sent, self.kept = [], []

    def send(self, src, dst, to):
        i = len(self.sent)
        copy = pltpu.make_async_remote_copy(
            src_ref=src,
            dst_ref=dst,
            send_sem=self.send_sems.at[i],
            recv_sem=self.recv_sems.at[i],
            device_id=device_of(to),
            device_id_type=pl.DeviceIdType.MESH,
        )
        copy.start()
        self.sent.append([copy, False])
        return i

    def local(self, src, dst):
        copy = pltpu.make_async_copy(src, dst, self.local_sems.at[len(self.kept)])
        copy.start()
        self.kept.append(copy)

    def arrived(self, i):
        if not self.sent[i][1]:
            self.sent[i][0].wait_recv()
            self.sent[i][1] = True

    def finish(self):
        for copy in self.kept:
            copy.wait()
        for i in range(len(self.sent)):
            self.arrived(i)
        for copy, _ in self.sent:
            copy.wait_send()


def greet(peers):
    barrier = pltpu.get_barrier_semaphore()
    for peer in peers:
        pl.semaphore_signal(
            barrier, inc=1, device_id=device_of(peer), device_id_type=pl.DeviceIdType.MESH
        )
    pl.semaphore_wait(barrier, len(peers))


def exchange(name, cid, body, peers, in_spaces, ins, outs, aliases, sends, locals_=1):
    def kernel(*refs):
        in_refs = refs[: len(ins)]
        out_refs = refs[len(ins) : len(ins) + len(outs)]
        send_sems, recv_sems, local_sems = refs[len(ins) + len(outs) :]
        at = here()
        greet(peers(at))
        net = Net(send_sems, recv_sems, local_sems)
        body(at, net, in_refs, out_refs)
        net.finish()

    return pl.pallas_call(
        kernel,
        out_shape=outs,
        in_specs=[pl.BlockSpec(memory_space=s) for s in in_spaces],
        out_specs=[pl.BlockSpec(memory_space=pltpu.HBM) for _ in outs],
        scratch_shapes=[
            pltpu.SemaphoreType.DMA((sends,)),
            pltpu.SemaphoreType.DMA((sends,)),
            pltpu.SemaphoreType.DMA((max(1, locals_),)),
        ],
        input_output_aliases=aliases,
        compiler_params=pltpu.CompilerParams(collective_id=cid, has_side_effects=True),
        name=name,
    )(*ins)


V = pltpu.VMEM
H = pltpu.HBM
LEFT = (1, 2, 3)
T1, T2 = 256, 384


def spread(features, places, merger_piece, llm_piece, bias_rows, text):
    tokens, depth = features.shape
    cols = merger_piece.shape[0]
    heads2, wide, rows = llm_piece.shape[1:]

    def peers(at):
        return (
            [moved(at, z=d) for d in LEFT]
            + [moved(at, x=d) for d in LEFT]
            + [moved(at, y=d) for d in LEFT]
            + [moved(at, k=1)]
        )

    def body(at, net, i, o):
        feat, place, merger, llm, bias, txt = i
        feat_all, place_all, merger_all, bias_all, llm_all, txt_all = o
        z, x, k, y = at["z"], at["x"], at["k"], at["y"]
        mine = x * 2 + k
        passing = []
        for d in LEFT:
            net.send(feat, feat_all.at[z], moved(at, z=d))
            net.send(place, place_all.at[z], moved(at, z=d))
            passing.append(net.send(merger, merger_all.at[mine], moved(at, x=d)))
            to = moved(at, y=d)
            net.send(llm.at[to["y"]], llm_all.at[y, :, z, x, k], to)
            net.send(bias, bias_all.at[y], to)
        net.send(merger, merger_all.at[mine], moved(at, k=1))
        for d in LEFT:
            net.send(txt.at[:T1], txt_all.at[y, :T1], moved(at, y=d))
        net.local(feat, feat_all.at[z])
        net.local(place, place_all.at[z])
        net.local(merger, merger_all.at[mine])
        net.local(llm.at[y], llm_all.at[y, :, z, x, k])
        net.local(bias, bias_all.at[y])
        net.local(txt, txt_all.at[y])
        for d, n in zip(LEFT, passing):
            net.arrived(n)
            source = ((x + 4 - d) % 4) * 2 + k
            net.send(merger_all.at[source], merger_all.at[source], moved(at, k=1))

    sds = jax.ShapeDtypeStruct
    return exchange(
        "spread",
        1,
        body,
        peers,
        [V] * 6,
        (features, places, merger_piece, llm_piece, bias_rows, text),
        (
            sds((NZ, tokens, depth), BF),
            sds((NZ,) + places.shape, jnp.int32),
            sds((NX * 2, cols, depth), BF),
            sds((NY,) + bias_rows.shape, F32),
            sds((NY, heads2, NZ, NX, 2, wide, rows), BF),
            sds((NY,) + text.shape, BF),
        ),
        {},
        15 + 1 + 3 + 3,
        6,
    )


def reduce_y(partial, llm_all):
    def peers(at):
        return [moved(at, y=d) for d in LEFT] + [moved(at, z=d) for d in LEFT]

    def body(at, net, i, o):
        part, _ = i
        got, llm = o
        z, x, k = at["z"], at["x"], at["k"]
        for d in LEFT:
            to = moved(at, y=d)
            net.send(part.at[to["y"]], got.at[d - 1], to)
        for d in LEFT:
            net.send(llm.at[:, :, z, x, k], llm.at[:, :, z, x, k], moved(at, z=d))

    sds = jax.ShapeDtypeStruct
    return exchange(
        "reduce_y",
        2,
        body,
        peers,
        [V, H],
        (partial, llm_all),
        (sds((3,) + partial.shape[1:], BF), sds(llm_all.shape, BF)),
        {1: 1},
        6,
    )


def reduce_h(half, llm_all, text, txt_all):
    def peers(at):
        return (
            [moved(at, h=1)]
            + [moved(at, x=d) for d in (1, 3)]
            + [moved(at, y=d) for d in LEFT]
        )

    def body(at, net, i, o):
        part, _, txt, _ = i
        got, llm, txt_all_ = o
        x, k, y = at["x"], at["k"], at["y"]
        net.send(part, got, moved(at, h=1))
        for d in (1, 3):
            piece = llm.at[:, :, pl.ds(0, 2), x, k]
            net.send(piece, piece, moved(at, x=d))
        for d in LEFT:
            net.send(txt.at[T1:T2], txt_all_.at[y, T1:T2], moved(at, y=d))

    sds = jax.ShapeDtypeStruct
    return exchange(
        "reduce_h",
        3,
        body,
        peers,
        [V, H, V, H],
        (half, llm_all, text, txt_all),
        (sds(half.shape, BF), sds(llm_all.shape, BF), sds(txt_all.shape, BF)),
        {1: 1, 3: 2},
        6,
    )


OTHERS = [(a, b, e) for a in range(4) for b in range(4) for e in range(2) if (a, b, e) != (0, 0, 0)]


def route(packed, llm_all, text, txt_all):
    def peers(at):
        return [moved(at, z=a, x=b, k=e) for a, b, e in OTHERS] + [moved(at, y=d) for d in LEFT]

    def body(at, net, i, o):
        pack, _, txt, _ = i
        got, llm, txt_all_ = o
        z, x, k, y = at["z"], at["x"], at["k"], at["y"]
        mine = got.at[z, x * 2 + k]
        for a, b, e in OTHERS:
            to = moved(at, z=a, x=b, k=e)
            net.send(pack.at[to["z"] * 8 + to["x"] * 2 + to["k"]], mine, to)
        for d in (1, 3):
            piece = llm.at[:, :, pl.ds(2, 2), x, k]
            net.send(piece, piece, moved(at, x=d))
        for d in LEFT:
            net.send(txt.at[T2:], txt_all_.at[y, T2:], moved(at, y=d))
        net.local(pack.at[z * 8 + x * 2 + k], mine)

    sds = jax.ShapeDtypeStruct
    return exchange(
        "route",
        4,
        body,
        peers,
        [V, H, V, H],
        (packed, llm_all, text, txt_all),
        (
            sds((NZ, NX * 2) + packed.shape[1:], BF),
            sds(llm_all.shape, BF),
            sds(txt_all.shape, BF),
        ),
        {1: 1, 3: 2},
        len(OTHERS) + 5,
    )


def collect(image, llm_all):
    def peers(at):
        return (
            [moved(at, y=d) for d in LEFT] + [moved(at, x=d) for d in (1, 3)] + [moved(at, k=1)]
        )

    def body(at, net, i, o):
        img, _ = i
        got, llm = o
        x, k, y = at["x"], at["k"], at["y"]
        for d in LEFT:
            net.send(img, got.at[:, y], moved(at, y=d))
        far = []
        for d, first in ((1, 0), (3, 2)):
            piece = llm.at[:, :, pl.ds(first, 2), (x + 4 - d) % 4, k]
            far.append(net.send(piece, piece, moved(at, x=d)))
        for step in (0, 1, 3):
            piece = llm.at[:, :, :, (x + step) % 4, k]
            net.send(piece, piece, moved(at, k=1))
        net.local(img, got.at[:, y])
        for n, first in zip(far, (0, 2)):
            net.arrived(n)
            piece = llm.at[:, :, pl.ds(first, 2), (x + 2) % 4, k]
            net.send(piece, piece, moved(at, k=1))

    sds = jax.ShapeDtypeStruct
    return exchange(
        "collect",
        5,
        body,
        peers,
        [V, H],
        (image, llm_all),
        (sds((image.shape[0], NY) + image.shape[1:], BF), sds(llm_all.shape, BF)),
        {1: 1},
        3 + 2 + 3 + 2,
    )


def ahead(at, steps):
    place = (at["z"] * 8 + at["x"] * 2 + at["k"] + 32 + steps) % 32
    return {"z": place // 8, "x": (place // 2) % 4, "k": place % 2, "y": at["y"], "h": at["h"]}


NEG = -1e30
QT = 128


def finish(slots, txt_all, weights, table, covered, bias, cosine, sine, seg_col, seg_row):
    blocks, tokens, width = txt_all.shape
    count = slots.shape[1]
    columns = weights.shape[2]
    qcols = GROUP * HD
    kvcols = 2 * HD

    def kernel(
        slots_h,
        txt_h,
        w_h,
        table_ref,
        cov_ref,
        bias_ref,
        cos_ref,
        sin_ref,
        segc_ref,
        segr_ref,
        out_ref,
        slots_v,
        hid,
        w_v,
        sq,
        sq_send,
        sq_got,
        kv_keep,
        kv_send,
        kv_got,
        q_keep,
        q_send,
        q_got,
        q_rot,
        kv,
        segs,
        m_s,
        l_s,
        acc,
        send_sems,
        recv_sems,
        local_sems,
    ):
        at = here()
        h = at["h"]
        c = lax.axis_index("ctx")
        loads = []

        def load(src, dst):
            copy = pltpu.make_async_copy(src, dst, local_sems.at[len(loads)])
            copy.start()
            loads.append(copy)

        load(slots_h, slots_v)
        for b in range(blocks):
            load(txt_h.at[b], hid.at[b])
        for b in range(blocks):
            load(w_h.at[b], w_v.at[b])
        load(segr_ref, segs.at[0])
        greet([ahead(at, s) for s in (1, 2, 3, 4, -1, -2, -3, -4)] + [moved(at, h=1)])
        net = Net(send_sems, recv_sems, local_sems)
        partner = moved(at, h=1)
        sibling = moved(at, k=1)
        seg_sent = [net.send(segr_ref, segs.at[s], ahead(at, s)) for s in range(1, REACH + 1)]
        sq[...] = jnp.zeros_like(sq)
        loads[0].wait()
        step = 256
        for b in range(blocks):
            loads[1 + b].wait()

            @pl.loop(0, tokens // step)
            def _(r, b=b):
                rows = pl.ds(pl.multiple_of(r * step, step), step)
                chosen = table_ref[rows, :]
                inside = cov_ref[rows, :] > 0.5
                total = jnp.zeros((step, 1), F32)
                for n in range(0, width, 512):
                    filled = jnp.dot(
                        chosen, slots_v[b, :, n : n + 512], preferred_element_type=F32
                    )
                    text = hid[b, rows, n : n + 512].astype(F32)
                    both = jnp.where(inside, filled, text)
                    hid[b, rows, n : n + 512] = both.astype(BF)
                    total = total + jnp.sum(both * both, axis=1, keepdims=True)
                sq[rows, :] = sq[rows, :] + total

        for b in range(blocks):
            loads[1 + blocks + b].wait()
        loads[1 + 2 * blocks].wait()
        sq_send[...] = jnp.broadcast_to(sq[...], (tokens, 128)).T[:8]

        def project(half, first_col, cols, store):
            per_row = cols // 256

            @pl.loop(0, (tokens // step) * per_row)
            def _(i):
                rows = pl.ds(pl.multiple_of((i // per_row) * step, step), step)
                inner = pl.multiple_of((i % per_row) * 256, 256)
                total = None
                for b in range(blocks):
                    part = lax.dot_general(
                        hid[b, rows, :],
                        w_v[b, half, pl.ds(first_col + inner, 256), :],
                        (((1,), (1,)), ((), ())),
                        preferred_element_type=F32,
                    )
                    total = part if total is None else total + part
                store[rows, pl.ds(inner, 256)] = total.astype(store.dtype)

        project(1 - h, qcols, kvcols, kv_send)
        kv_n = net.send(kv_send, kv_got, partner)
        sq_n = net.send(sq_send, sq_got, partner)
        project(1 - h, 0, qcols, q_send)
        q_n = net.send(q_send, q_got, partner)
        project(h, qcols, kvcols, kv_keep)

        net.arrived(sq_n)
        net.arrived(kv_n)
        other = jnp.broadcast_to(sq_got[:1, :], (128, tokens)).T[:, :1]
        sq[...] = lax.rsqrt((sq[...] + other) * (1.0 / D) + RMS_EPS)

        def turned(u, rows):
            return u * cos_ref[rows, :] + pltpu.roll(u, HD // 2, 1) * sin_ref[rows, :]

        @pl.loop(0, tokens // QT)
        def _(r):
            rows = pl.ds(pl.multiple_of(r * QT, QT), QT)
            both = (kv_keep[rows, :] + kv_got[rows, :].astype(F32)) * sq[rows, :]
            both = both + bias_ref[:, qcols:]
            kv[0, rows, :HD] = turned(both[:, :HD], rows).astype(BF)
            kv[0, rows, HD:] = both[:, HD:].astype(BF)

        near = net.send(kv.at[0], kv.at[2], ahead(at, 2))
        far = net.send(kv.at[0], kv.at[4], ahead(at, 4))
        project(h, 0, qcols, q_keep)
        net.arrived(near)
        one = net.send(kv.at[2 * at["k"]], kv.at[1], sibling)
        net.arrived(far)
        three = net.send(kv.at[2 + 2 * at["k"]], kv.at[3], sibling)
        net.arrived(q_n)

        @pl.loop(0, tokens // QT)
        def _(r):
            rows = pl.ds(pl.multiple_of(r * QT, QT), QT)
            for j in range(GROUP):
                lanes = slice(j * HD, (j + 1) * HD)
                u = (q_keep[rows, lanes] + q_got[rows, lanes].astype(F32)) * sq[rows, :]
                u = u + bias_ref[:, lanes]
                q_rot[j, rows, :] = turned(u, rows).astype(BF)

        factor = HD ** (-0.5) * 1.4426950408889634

        def attend(d, start):
            @pl.loop(0, tokens // QT)
            def _(r):
                rows = pl.ds(pl.multiple_of(r * QT, QT), QT)
                key_seg = jnp.where(c >= d, segs[d, :1, :], -1)
                allowed = segc_ref[rows, :] == key_seg
                if d == 0:
                    q_at = lax.broadcasted_iota(jnp.int32, (QT, tokens), 0) + r * QT
                    k_at = lax.broadcasted_iota(jnp.int32, (QT, tokens), 1)
                    allowed = allowed & (k_at <= q_at)
                for j in range(GROUP):
                    scores = lax.dot_general(
                        q_rot[j, rows, :],
                        kv[d, :, :HD],
                        (((1,), (1,)), ((), ())),
                        preferred_element_type=F32,
                    )
                    scores = jnp.where(allowed, scores * factor, NEG)
                    top = jnp.max(scores, axis=1, keepdims=True)
                    if not start:
                        before = m_s[j, rows, :]
                        top = jnp.maximum(before, top)
                    raised = jnp.exp2(scores - top)
                    total = jnp.sum(raised, axis=1, keepdims=True)
                    blended = jnp.dot(
                        raised.astype(BF), kv[d, :, HD:], preferred_element_type=F32
                    )
                    if not start:
                        fade = jnp.exp2(before - top)
                        total = total + fade * l_s[j, rows, :]
                        blended = blended + fade * acc[j, rows, :]
                    m_s[j, rows, :] = top
                    l_s[j, rows, :] = total
                    acc[j, rows, :] = blended

        attend(0, True)
        for n in seg_sent:
            net.arrived(n)
        attend(2, False)
        attend(4, False)
        net.arrived(one)
        attend(1, False)
        net.arrived(three)
        attend(3, False)

        @pl.loop(0, tokens // QT)
        def _(r):
            rows = pl.ds(pl.multiple_of(r * QT, QT), QT)
            for j in range(GROUP):
                out_ref[rows, j * HD : (j + 1) * HD] = (
                    acc[j, rows, :] / l_s[j, rows, :]
                ).astype(BF)

        net.finish()

    sends = REACH + 3 + 2 + 2
    vm = pltpu.VMEM
    spaces = [H, H, H] + [V] * 7
    return pl.pallas_call(
        kernel,
        out_shape=jax.ShapeDtypeStruct((tokens, qcols), BF),
        in_specs=[pl.BlockSpec(memory_space=s) for s in spaces],
        out_specs=pl.BlockSpec(memory_space=V),
        scratch_shapes=[
            vm(slots.shape, BF),
            vm(txt_all.shape, BF),
            vm(weights.shape, BF),
            vm((tokens, 1), F32),
            vm((8, tokens), F32),
            vm((8, tokens), F32),
            vm((tokens, kvcols), F32),
            vm((tokens, kvcols), BF),
            vm((tokens, kvcols), BF),
            vm((tokens, qcols), F32),
            vm((tokens, qcols), BF),
            vm((tokens, qcols), BF),
            vm((GROUP, tokens, HD), BF),
            vm((REACH + 1, tokens, kvcols), BF),
            vm((REACH + 1, 8, tokens), jnp.int32),
            vm((GROUP, tokens, 1), F32),
            vm((GROUP, tokens, 1), F32),
            vm((GROUP, tokens, HD), F32),
            pltpu.SemaphoreType.DMA((sends,)),
            pltpu.SemaphoreType.DMA((sends,)),
            pltpu.SemaphoreType.DMA((2 + 2 * blocks,)),
        ],
        compiler_params=pltpu.CompilerParams(
            collective_id=6, has_side_effects=True, vmem_limit_bytes=60 << 20
        ),
        name="finish",
    )(slots, txt_all, weights, table, covered, bias, cosine, sine, seg_col, seg_row)


def softmax_rows(scores, allowed):
    masked = jnp.where(allowed, scores, FILL_LOW)
    highest = jnp.max(masked, axis=-1, keepdims=True)
    raised = jnp.exp(masked - highest)
    return raised / jnp.sum(raised, axis=-1, keepdims=True)


def vision_norm_rows(patches, vit_gain):
    values = patches.astype(F32)
    mean_square = jnp.mean(values * values, axis=1, keepdims=True)
    return (values * lax.rsqrt(mean_square + VIT_EPS) * vit_gain).astype(BF)


def window_attention(normed, weight_block, bias_block, window_ids):
    row_count = normed.shape[0]
    packed = jnp.dot(
        normed, weight_block.reshape(normed.shape[1], -1), preferred_element_type=F32
    )
    triple = (packed.reshape(row_count, 3, -1) + bias_block).astype(BF)
    heads_here = triple.shape[2] // VHD
    queries = triple[:, 0].reshape(row_count, heads_here, VHD)
    keys_here = triple[:, 1].reshape(row_count, heads_here, VHD)
    values_here = triple[:, 2].reshape(row_count, heads_here, VHD)
    scores = jnp.einsum(
        "qhd,khd->hqk", queries, keys_here, preferred_element_type=F32
    ) * VHD ** (-0.5)
    allowed = window_ids[:, None] == window_ids[None, :]
    softmaxed = softmax_rows(scores, allowed[None]).astype(BF)
    blended = jnp.einsum("hqk,khd->qhd", softmaxed, values_here, preferred_element_type=F32)
    return blended.astype(BF).reshape(row_count, -1)


def rope_tables(first, length):
    places = (first + jnp.arange(length, dtype=jnp.int32)).astype(F32)
    frequency = ROPE_BASE ** (-jnp.arange(0, HD, 2).astype(F32) / HD)
    angles = places[:, None] * frequency[None, :]
    angles = jnp.concatenate([angles, angles], axis=1)
    return (jnp.cos(angles), jnp.sin(angles))


def pack_tokens(values, positions, span, owners):
    items = values.shape[0]
    target = positions // span
    item_order = jnp.arange(items, dtype=jnp.int32)
    before = (target[None, :] == target[:, None]) & (item_order[None, :] < item_order[:, None])
    ranks = jnp.sum(before.astype(jnp.int32), axis=1)
    slots = target * CAP + ranks
    table = slots[None, :] == jnp.arange(owners * CAP, dtype=jnp.int32)[:, None]
    local = positions - target * span
    lanes = jnp.arange(HD)[None, :]
    notes = jnp.where(lanes == 0, (local // 16)[:, None], (local % 16)[:, None])
    notes = jnp.where(lanes == 2, 1, notes)
    rows = jnp.concatenate([values, notes.astype(BF)], axis=1)
    packed = jnp.dot(table.astype(BF), rows, preferred_element_type=F32).astype(BF)
    return packed.reshape(owners, CAP, rows.shape[1])


def on_device(
    patches,
    vit_gain,
    vit_codes,
    vit_scales,
    vit_bias,
    window_ids,
    merger_codes,
    merger_scales,
    merger_bias,
    positions,
    text_embed,
    norm_gain,
    llm_codes,
    llm_scales,
    llm_bias,
    segments,
):
    at = here()
    owners = lax.axis_size("ctx")
    row_count, width = text_embed.shape
    first = lax.axis_index("ctx") * row_count

    llm_weight = (llm_codes.astype(F32) * llm_scales.astype(F32)).astype(BF)
    llm_weight = (llm_weight.astype(F32) * norm_gain[:, None, None]).astype(BF)
    llm_piece = jnp.transpose(llm_weight, (1, 2, 0)).reshape(NY, 2, -1, width)
    merger_weight = (merger_codes.astype(F32) * merger_scales.astype(F32)).astype(BF)
    merger_piece = merger_weight.reshape(-1, merger_weight.shape[2]).T

    normed_patches = vision_norm_rows(patches, vit_gain)
    vit_weight = (vit_codes.astype(F32) * vit_scales.astype(F32)[0]).astype(BF)
    attended = window_attention(normed_patches, vit_weight, vit_bias, window_ids)
    token_count = positions.shape[0]
    features = attended.reshape(token_count, -1)
    place_rows = jnp.broadcast_to(positions[None, :], (8, token_count))

    feat_all, place_all, merger_all, bias_all, llm_all, txt_all = spread(
        features, place_rows, merger_piece, llm_piece, merger_bias.reshape(8, -1), text_embed
    )
    product = lax.dot_general(
        feat_all.reshape(-1, feat_all.shape[2]),
        merger_all.reshape(-1, merger_all.shape[2]),
        (((1,), (1,)), ((), ())),
        preferred_element_type=F32,
    ).astype(BF)
    product = product.reshape(NZ, token_count, -1)
    got, llm_all = reduce_y(product, llm_all)
    total = lax.dynamic_index_in_dim(product, at["y"], 0, keepdims=False).astype(F32)
    total = total + got.astype(F32).sum(axis=0)
    low, high = (total[:, :width], total[:, width:])
    is_high = at["h"] == 1
    keep = jnp.where(is_high, high, low)
    give = jnp.where(is_high, low, high).astype(BF)
    got, llm_all, txt_all = reduce_h(give, llm_all, text_embed, txt_all)
    bias_here = lax.dynamic_index_in_dim(bias_all, at["z"], 0, keepdims=False).reshape(-1)
    merged = (keep + got.astype(F32) + bias_here).astype(BF)
    places_here = lax.dynamic_index_in_dim(place_all, at["y"], 0, keepdims=False)[0]
    packed = pack_tokens(merged, places_here, row_count, owners)
    image, llm_all, txt_all = route(packed, llm_all, text_embed, txt_all)
    image = image.reshape(NZ, -1, image.shape[3])
    slots, llm_all = collect(image, llm_all)
    slots = slots.reshape(NZ, -1, slots.shape[3])

    notes = slots[0, :, width : width + 3].astype(F32)
    local = jnp.where(notes[:, 2] > 0.5, notes[:, 0] * 16.0 + notes[:, 1], -1.0).astype(jnp.int32)
    table = local[None, :] == jnp.arange(row_count, dtype=jnp.int32)[:, None]
    filled = jnp.stack(
        [
            jnp.dot(table.astype(BF), slots[b, :, :width], preferred_element_type=F32).astype(BF)
            for b in range(NY)
        ]
    )
    covered = jnp.any(table, axis=1, keepdims=True).astype(F32)
    cosine, sine = rope_tables(first, row_count)
    sine = jnp.where(jnp.arange(HD)[None, :] < HD // 2, -sine, sine)
    seg_row = jnp.broadcast_to(segments[None, :], (8, row_count))
    return finish(
        slots,
        txt_all,
        llm_all.reshape(NY, 2, -1, width),
        table.astype(BF),
        covered,
        llm_bias,
        cosine,
        sine,
        segments[:, None],
        seg_row,
    )


def solution(mesh):
    in_specs = (
        P("ctx", None),
        P(),
        P(None, None, "wt"),
        P("wt"),
        P(None, "wt"),
        P("ctx"),
        P(None, "wt", "ctx"),
        P(None, "wt", "ctx"),
        P("wt"),
        P("ctx"),
        P("ctx", "wt"),
        P("wt"),
        P("wt", None, "ctx"),
        P("wt", None, "ctx"),
        P("wt", None),
        P("ctx"),
    )
    out_specs = P("ctx", "wt")
    return jax.shard_map(
        on_device, mesh=mesh, in_specs=in_specs, out_specs=out_specs, check_vma=False
    )
```
